256 devices in a mesh: tm: 32 (over z_lo, x, core), lat: 8 (over z_hi, y).
Axes of the slice: x: 4, y: 4, z: 8 (z_hi: 2, z_lo: 4; z = z_hi * 4 + z_lo), core: 2. Of those that a mesh axis runs over, the one named last changes fastest.
Arguments:
- first_guess: float32 [32, 69, 64, 512], P('tm', None, 'lat'), may hold values from -6 to 6
- background: float32 [69, 64, 512], P(None, 'lat'), may hold values from -6 to 6
- observed: float32 [32, 69, 64, 512], P('tm', None, 'lat'), may hold values from -6 to 6
- cell_mask: int32 [32, 64, 512], P('tm', 'lat'), may hold values 0 or 1
- chan_mask: int32 [32, 69], P('tm'), may hold values 0 or 1
- w_in: bfloat16 [9, 128, 69], replicated, may hold values from -0.25 to 0.25
- b_in: float32 [128], replicated, may hold values from -3 to 3
- w_out: bfloat16 [9, 69, 128], replicated, may hold values from -0.1875 to 0.1875
Outputs:
- analysis: float32 [32, 69, 64, 512], P('tm', None, 'lat')
The draws below stay inside these ranges and needn't reach their ends.
All inputs are finite; a program needn't handle non-finite values. No bound on the sum of `cell_mask` or of `chan_mask` on one device may be relied on, other than what follows from the above.
Results may differ from the reference program's by a relative error of at most 0.0037.
Values may be sent and summed in bfloat16 or wider, within the bound.
No kernel may reach another device: no remote copies, remote signals or barrier semaphores. Data moves between devices by JAX's collectives and lax.ppermute only.
A program may use at most 64 MiB of HBM per device.

```python
import jax
import jax.numpy as jnp
from jax import lax

C = 69
HID = 128
LON = 512
ITERS = 2
SUBWIN = 32
LATS = 64


def place_ends(drawn, rng, smallest, high):
    place = [jax.random.randint(jax.random.fold_in(rng, axis), (), 0, length) for axis, length in enumerate(drawn.shape)]
    longest = drawn.shape.index(max(drawn.shape))
    next_to = place[:longest] + [(place[longest] + 1) % drawn.shape[longest]] + place[longest + 1:]
    return drawn.at[tuple(place)].set(smallest).at[tuple(next_to)].set(high)


def block_levels(key, extent, split, low, high):
    def one(dim, blocks):
        heights = jax.random.uniform(jax.random.fold_in(jax.random.fold_in(key, 6), dim), (blocks,), jnp.float32, low / len(split), high / len(split))
        return jnp.repeat(jnp.exp(heights), extent[dim] // blocks).reshape((-1,) + (1,) * (len(extent) - dim - 1))

    loudness = one(*split[0])
    for cut in split[1:]:
        loudness = loudness * one(*cut)
    return loudness


def bell_draw(own_key, shape, spread, bound, split=(), held_as=jnp.bfloat16):
    gain = block_levels(own_key, shape, split, -0.22, 0.18) if split else 1.0
    entries = jax.random.normal(own_key, shape, jnp.float32) * spread * gain
    return jnp.minimum(jnp.maximum(entries, -bound), bound).astype(held_as)


def setup_inputs(seed: int = 0) -> dict:
    seeds = jax.random.split(jax.random.key(seed), 9)
    first_guess = bell_draw(seeds[0], (SUBWIN, C, LATS, LON), 1.0, 6.0, ((0, 32), (2, 8)), jnp.float32)
    background = bell_draw(seeds[1], (C, LATS, LON), 1.0, 6.0, ((1, 8),), jnp.float32)
    observed = bell_draw(seeds[2], (SUBWIN, C, LATS, LON), 1.0, 6.0, ((0, 32), (2, 8)), jnp.float32)
    cell_mask = place_ends((jax.random.randint(seeds[3], (SUBWIN, LATS, LON), 0, 3) < 1).astype(jnp.int32), jax.random.fold_in(seeds[3], 1), 0, 1)
    chan_mask = place_ends((jax.random.randint(seeds[4], (SUBWIN, C), 0, 4) < 3).astype(jnp.int32), jax.random.fold_in(seeds[4], 1), 0, 1)
    w_in = bell_draw(seeds[5], (9, HID, C), (9 * C) ** -0.5, 0.25)
    b_in = bell_draw(seeds[6], (HID,), 0.5, 3.0, (), jnp.float32)
    w_out = bell_draw(seeds[7], (9, C, HID), (9 * HID) ** -0.5, 0.1875)
    return {"first_guess": first_guess, "background": background, "observed": observed, "cell_mask": cell_mask, "chan_mask": chan_mask, "w_in": w_in, "b_in": b_in, "w_out": w_out}


step_size = 0.25


def pad_rows(field):
    return jnp.pad(field, ((0, 0), (1, 1), (0, 0)))


def conv_apply(padded, weight):
    rows = padded.shape[1] - 2
    stacked = jnp.stack([jnp.roll(padded[:, 1 + dr:1 + dr + rows, :], -dl, axis=2) for dr in (-1, 0, 1) for dl in (-1, 0, 1)])
    return jnp.einsum("toi,tirl->orl", weight.astype(jnp.float32), stacked.astype(jnp.float32))


def conv_adjoint(padded, weight):
    rows = padded.shape[1] - 2
    stacked = jnp.stack([jnp.roll(padded[:, 1 - dr:1 - dr + rows, :], dl, axis=2) for dr in (-1, 0, 1) for dl in (-1, 0, 1)])
    return jnp.einsum("toi,torl->irl", weight.astype(jnp.float32), stacked.astype(jnp.float32))


def forward(state, w_in, b_in, w_out):
    xb = state.astype(jnp.bfloat16)
    hidden = conv_apply(pad_rows(xb), w_in) + b_in[:, None, None]
    act = jax.nn.silu(hidden).astype(jnp.bfloat16)
    return state + conv_apply(pad_rows(act), w_out), hidden


def adjoint(lam, hidden, w_in, w_out):
    lowered = lam.astype(jnp.bfloat16)
    grad_act = conv_adjoint(pad_rows(lowered), w_out)
    sig = jax.nn.sigmoid(hidden)
    grad_hidden = (grad_act * sig * (1.0 + hidden * (1.0 - sig))).astype(jnp.bfloat16)
    return conv_adjoint(pad_rows(grad_hidden), w_in)


def reference(first_guess, background, observed, cell_mask, chan_mask, w_in, b_in, w_out):
    state = first_guess
    weight = cell_mask[:, None, :, :].astype(jnp.float32) * chan_mask[:, :, None, None].astype(jnp.float32)
    for step in range(ITERS):
        fore, hidden = lax.map(lambda s: forward(s, w_in, b_in, w_out), state)
        earlier = jnp.concatenate([background[None], fore[:-1]], axis=0)
        err = state - earlier
        later = jnp.concatenate([err[1:], jnp.zeros_like(err[:1])], axis=0)
        lam = weight * (fore - observed) - later
        grad_in = lax.map(lambda pair: adjoint(pair[0], pair[1], w_in, w_out), (lam, hidden))
        state = state - step_size * (err + lam + grad_in)
    return state
```

```python
import functools

import jax
import jax.numpy as jnp
from jax import lax
from jax.experimental import pallas as pl
from jax.experimental.pallas import tpu as pltpu
from jax.sharding import PartitionSpec as P

ITERS = 2
STEP = 0.25
CF = 72
CB = 80
VMEM = pl.BlockSpec(memory_space=pltpu.VMEM)
SMEM = pl.BlockSpec(memory_space=pltpu.SMEM)


def pair_exchange(to_low, to_high, axis):
    count = lax.axis_size(axis)
    odd = lax.axis_index(axis) % 2 == 1
    first = [p for i in range(0, count - 1, 2) for p in ((i, i + 1), (i + 1, i))]
    second = [p for i in range(1, count - 1, 2) for p in ((i, i + 1), (i + 1, i))]
    far = lax.ppermute(jnp.where(odd, to_high, to_low), axis, second)
    near = lax.ppermute(jnp.where(odd, to_low, to_high), axis, first)
    return jnp.where(odd, near, far), jnp.where(odd, far, near)


def shifted_sum(y, rows):
    lon = y.shape[1]
    left = pltpu.roll(y[:rows], 1, 1)
    right = pltpu.roll(y[2 * rows :], lon - 1, 1)
    return y[rows : 2 * rows] + left + right


def pad_channels(v):
    return jnp.concatenate([v, jnp.zeros((CB - v.shape[0], v.shape[1]), v.dtype)], axis=0)


def place_rows(dst, lo, own, hi):
    n = own.shape[0]
    for i in range(2):
        dst[pl.ds(i * CB, CB), :] = lo[i]
        dst[pl.ds((n + 2 + i) * CB, CB), :] = hi[i]
    for r in range(n):
        dst[pl.ds((r + 2) * CB, CB), :] = own[r]


def window(ref, j, unit):
    return ref[pl.ds(pl.multiple_of(j * unit, unit), 3 * unit), :]


def forward_kernel(flags, lo, own, hi, state, obs, nxt, cell, chan, wup, bias, wdn,
                   fore_out, lb_out, slope_out, acc_out, xs, acts, chans):
    n, hid = own.shape[0], bias.shape[0]
    lon = own.shape[2]
    place_rows(xs, lo, own, hi)
    has_low, has_high, has_next = flags[0], flags[1], flags[2]
    chans[...] = jnp.broadcast_to(chan[...], chans.shape)

    def up(j, carry):
        y = jnp.dot(wup[...], window(xs, j, CB), preferred_element_type=jnp.float32)
        z = shifted_sum(y, hid) + bias[...]
        inside = jnp.where(j == 0, has_low, jnp.where(j == n + 1, has_high, 1.0))
        s = jax.nn.sigmoid(z)
        acts[pl.ds(pl.multiple_of(j * hid, hid), hid), :] = (z * s * inside).astype(jnp.bfloat16)
        slope_out[j] = (s * (1.0 + z * (1.0 - s)) * inside).astype(jnp.bfloat16)
        return carry

    lax.fori_loop(0, n + 2, up, 0)

    def down(r, carry):
        y = jnp.dot(wdn[...], window(acts, r, hid), preferred_element_type=jnp.float32)
        st = state[r]
        fore = st + shifted_sum(y, CF)
        fore_out[r] = fore.astype(jnp.bfloat16)
        w = chans[...] * cell[pl.ds(r, 1), :].astype(jnp.float32)
        lam = w * (fore - obs[r]) - has_next * (nxt[r].astype(jnp.float32) - fore)
        lb_out[r] = pad_channels(lam).astype(jnp.bfloat16)
        acc_out[r] = st - STEP * (st + lam)
        return carry

    lax.fori_loop(0, n, down, 0)


def adjoint_kernel(flags, lo, own, hi, slope, acc, prev, ground, wup, wdn,
                   state_out, xb_out, xs, grads):
    n, hid = own.shape[0], slope.shape[1]
    place_rows(xs, lo, own, hi)

    def up(j, carry):
        y = jnp.dot(wup[...], window(xs, j, CB), preferred_element_type=jnp.float32)
        g = shifted_sum(y, hid) * slope[j].astype(jnp.float32)
        grads[pl.ds(pl.multiple_of(j * hid, hid), hid), :] = g.astype(jnp.bfloat16)
        return carry

    lax.fori_loop(0, n + 2, up, 0)
    first = flags[3] > 0.5

    def down(r, carry):
        y = jnp.dot(wdn[...], window(grads, r, hid), preferred_element_type=jnp.float32)
        earlier = jnp.where(first, ground[r], prev[r].astype(jnp.float32))
        st = acc[r] + STEP * (earlier - shifted_sum(y, CF))
        state_out[r] = st
        xb_out[r] = pad_channels(st).astype(jnp.bfloat16)
        return carry

    lax.fori_loop(0, n, down, 0)


def stack_taps(w, out_pad, in_pad):
    w = jnp.pad(w, ((0, 0), (0, out_pad - w.shape[1]), (0, in_pad - w.shape[2])))
    w = w.reshape(3, 3, out_pad, in_pad)
    return w.transpose(1, 2, 0, 3).reshape(3 * out_pad, 3 * in_pad)


def adjoint_taps(w):
    return jnp.flip(w, 0).transpose(0, 2, 1)


def by_rows(x, pad):
    x = x.transpose(1, 0, 2)
    return jnp.pad(x, ((0, 0), (0, pad - x.shape[1]), (0, 0)))


def local(first_guess, background, observed, cell_mask, chan_mask, w_in, b_in, w_out):
    c, n, lon = first_guess.shape[1:]
    hid = b_in.shape[0]
    f32, bf16 = jnp.float32, jnp.bfloat16
    lat, lats = lax.axis_index("lat"), lax.axis_size("lat")
    tm, tms = lax.axis_index("tm"), lax.axis_size("tm")
    flags = jnp.stack([lat > 0, lat < lats - 1, tm < tms - 1, tm == 0]).astype(f32)
    state = by_rows(first_guess[0], CF)
    xb = by_rows(first_guess[0].astype(bf16), CB)
    obs = by_rows(observed[0], CF)
    ground = by_rows(background, CF)
    cell = cell_mask[0]
    chan = jnp.pad(chan_mask[0].astype(f32), (0, CF - c))[:, None]
    up1, dn1 = stack_taps(w_in, hid, CB), stack_taps(w_out, CF, hid)
    up2, dn2 = stack_taps(adjoint_taps(w_out), hid, CB), stack_taps(adjoint_taps(w_in), CF, hid)
    bias = b_in[:, None]
    S = jax.ShapeDtypeStruct
    params = pltpu.CompilerParams(vmem_limit_bytes=40 * 2**20)
    fwd = pl.pallas_call(
        forward_kernel,
        out_shape=(S((n, CF, lon), bf16), S((n, CB, lon), bf16), S((n + 2, hid, lon), bf16), S((n, CF, lon), f32)),
        in_specs=[SMEM] + [VMEM] * 11,
        out_specs=(VMEM,) * 4,
        scratch_shapes=[pltpu.VMEM(((n + 4) * CB, lon), bf16), pltpu.VMEM(((n + 2) * hid, lon), bf16), pltpu.VMEM((CF, lon), f32)],
        compiler_params=params,
        name="forward",
    )
    adj = pl.pallas_call(
        adjoint_kernel,
        out_shape=(S((n, CF, lon), f32), S((n, CB, lon), bf16)),
        in_specs=[SMEM] + [VMEM] * 9,
        out_specs=(VMEM,) * 2,
        scratch_shapes=[pltpu.VMEM(((n + 4) * CB, lon), bf16), pltpu.VMEM(((n + 2) * hid, lon), bf16)],
        compiler_params=params,
        name="adjoint",
    )
    ahead = [(i, i + 1) for i in range(tms - 1)]
    back = [(j, i) for i, j in ahead]
    for _ in range(ITERS):
        lo, hi = pair_exchange(xb[:2], xb[n - 2 :], "lat")
        nxt = lax.ppermute(xb[:, :CF], "tm", back)
        fore, lb, slope, acc = fwd(flags, lo, xb, hi, state, obs, nxt, cell, chan, up1, bias, dn1)
        lo, hi = pair_exchange(lb[:2], lb[n - 2 :], "lat")
        prev = lax.ppermute(fore, "tm", ahead)
        state, xb = adj(flags, lo, lb, hi, slope, acc, prev, ground, up2, dn2)
    return state[:, :c].transpose(1, 0, 2)[None]


def solution(mesh):
    return jax.shard_map(
        local,
        mesh=mesh,
        in_specs=(
            P("tm", None, "lat", None),
            P(None, "lat", None),
            P("tm", None, "lat", None),
            P("tm", "lat", None),
            P("tm", None),
            P(),
            P(),
            P(),
        ),
        out_specs=P("tm", None, "lat", None),
        check_vma=False,
    )
```

```python
import jax
import jax.numpy as jnp
from jax import lax
from jax.experimental import pallas as pl
from jax.experimental.pallas import tpu as pltpu
from jax.sharding import PartitionSpec as P

ITERS = 2
STEP = 0.25
CF = 72
CB = 80
VMEM = pl.BlockSpec(memory_space=pltpu.VMEM)
SMEM = pl.BlockSpec(memory_space=pltpu.SMEM)
F32, BF16 = jnp.float32, jnp.bfloat16


def dot(a, b):
    return jnp.dot(a, b, preferred_element_type=F32)


def shifted_sum(y):
    lon = y.shape[1]
    left = pltpu.roll(y[:CF], 1, 1)
    right = pltpu.roll(y[2 * CF :], lon - 1, 1)
    return y[CF : 2 * CF] + left + right


def place_row(dst, j, row):
    x = row.astype(F32)
    lon = x.shape[1]
    pad = jnp.zeros((CB - x.shape[0], lon), F32)
    for i, v in enumerate((pltpu.roll(x, 1, 1), x, pltpu.roll(x, lon - 1, 1))):
        dst[pl.ds((3 * j + i) * CB, CB), :] = jnp.concatenate([v, pad], axis=0).astype(BF16)


def window(ref, j, unit):
    return ref[pl.ds(j * unit, 3 * unit), :]


def halos(flags, far, near, i):
    odd = flags[4] > 0.5
    a, b = far[i].astype(F32), near[i].astype(F32)
    return jnp.where(odd, b, a), jnp.where(odd, a, b)


def send_edges(flags, rows, far_out, near_out):
    odd = flags[4] > 0.5
    for i in range(2):
        low, high = rows[i], rows[2 + i]
        far_out[i] = jnp.where(odd, high, low).astype(BF16)
        near_out[i] = jnp.where(odd, low, high).astype(BF16)


def inner_forward(own, state, wup, bias, wdn, fore_out, acts_out, slope_out, xs, acts):
    n, hid = own.shape[0], bias.shape[0]

    def up(j):
        z = dot(wup[...], window(xs, j - 1, 3 * CB)) + bias[...]
        s = jax.nn.sigmoid(z)
        act = z * s
        slope_out[j - 1] = (s + act * (1.0 - s)).astype(BF16)
        act = act.astype(BF16)
        acts[pl.ds((j - 1) * hid, hid), :] = act
        if j in (1, 2):
            acts_out[j - 1] = act
        if j in (n - 3, n - 2):
            acts_out[j - n + 5] = act

    def down(r):
        fore_out[r - 2] = state[r] + shifted_sum(dot(wdn[...], window(acts, r - 2, hid)))

    place_row(xs, 0, own[0])
    place_row(xs, 1, own[1])
    for j in range(1, n - 1):
        place_row(xs, j + 1, own[j + 1])
        up(j)
        if j >= 3:
            down(j - 1)


def edge_forward(flags, far, near, own, inner, inner_acts, state, obs, nxt, cell, chan, wup, bias, wdn,
                 fore_out, lb_out, far_out, near_out, slope_out, acc_out, xs, acts, chans):
    n, hid = own.shape[0], bias.shape[0]
    has_low, has_high, has_next = flags[0], flags[1], flags[2]
    chans[...] = jnp.broadcast_to(chan[...], chans.shape)
    for i in range(2):
        below, above = halos(flags, far, near, i)
        place_row(xs, i, below)
        place_row(xs, 2 + i, own[i])
        place_row(xs, 4 + i, own[n - 2 + i])
        place_row(xs, 6 + i, above)
        acts[pl.ds((2 + i) * hid, hid), :] = inner_acts[i]
        acts[pl.ds((4 + i) * hid, hid), :] = inner_acts[2 + i]

    def up(x_at, act_at, slope_at, inside):
        z = dot(wup[...], window(xs, x_at, 3 * CB)) + bias[...]
        s = jax.nn.sigmoid(z)
        act = z * s
        slope = s + act * (1.0 - s)
        if inside is not None:
            act, slope = act * inside, slope * inside
        acts[pl.ds(act_at * hid, hid), :] = act.astype(BF16)
        slope_out[slope_at] = slope.astype(BF16)

    def finish(r, fore):
        st = state[r]
        fore_out[r] = fore.astype(BF16)
        w = chans[...] * cell[pl.ds(r, 1), :].astype(F32)
        lam = w * (fore - obs[r]) - has_next * (nxt[r].astype(F32) - fore)
        lb_out[r] = lam.astype(BF16)
        acc_out[r] = st - STEP * (st + lam)
        return lam

    up(0, 0, 0, has_low)
    up(1, 1, 1, None)
    up(4, 6, 2, None)
    up(5, 7, 3, has_high)
    edges = [
        finish(r, state[r] + shifted_sum(dot(wdn[...], window(acts, at, hid))))
        for r, at in ((0, 0), (1, 1), (n - 2, 4), (n - 1, 5))
    ]
    send_edges(flags, edges, far_out, near_out)
    for r in range(2, n - 2):
        finish(r, inner[r - 2])


def inner_adjoint(own, slope, wup, wdn, grad_out, rows_out, xs, grads):
    n, hid = own.shape[0], slope.shape[1]

    def up(j):
        g = (dot(wup[...], window(xs, j - 1, 3 * CB)) * slope[j - 1].astype(F32)).astype(BF16)
        grads[pl.ds((j - 1) * hid, hid), :] = g
        if j in (1, 2):
            rows_out[j - 1] = g
        if j in (n - 3, n - 2):
            rows_out[j - n + 5] = g

    def down(r):
        grad_out[r - 2] = shifted_sum(dot(wdn[...], window(grads, r - 2, hid)))

    place_row(xs, 0, own[0])
    place_row(xs, 1, own[1])
    for j in range(1, n - 1):
        place_row(xs, j + 1, own[j + 1])
        up(j)
        if j >= 3:
            down(j - 1)


def edge_adjoint(flags, far, near, own, inner, inner_rows, slope, acc, prev, ground, wup, wdn,
                 state_out, xb_out, far_out, near_out, xs, grads):
    n, hid = own.shape[0], slope.shape[1]
    first = flags[3] > 0.5
    for i in range(2):
        below, above = halos(flags, far, near, i)
        place_row(xs, i, below)
        place_row(xs, 2 + i, own[i])
        place_row(xs, 4 + i, own[n - 2 + i])
        place_row(xs, 6 + i, above)
        grads[pl.ds((2 + i) * hid, hid), :] = inner_rows[i]
        grads[pl.ds((4 + i) * hid, hid), :] = inner_rows[2 + i]

    def up(x_at, at, slope_at):
        g = dot(wup[...], window(xs, x_at, 3 * CB)) * slope[slope_at].astype(F32)
        grads[pl.ds(at * hid, hid), :] = g.astype(BF16)

    def finish(r, grad):
        earlier = jnp.where(first, ground[r], prev[r].astype(F32))
        st = acc[r] + STEP * (earlier - grad)
        state_out[r] = st
        xb_out[r] = st.astype(BF16)
        return st

    up(0, 0, 0)
    up(1, 1, 1)
    up(4, 6, 2)
    up(5, 7, 3)
    edges = [
        finish(r, shifted_sum(dot(wdn[...], window(grads, at, hid))))
        for r, at in ((0, 0), (1, 1), (n - 2, 4), (n - 1, 5))
    ]
    send_edges(flags, edges, far_out, near_out)
    for r in range(2, n - 2):
        finish(r, inner[r - 2])


def stack_out(w):
    w = jnp.pad(w, ((0, 0), (0, CF - w.shape[1]), (0, 0))).reshape(3, 3, CF, w.shape[2])
    return w.transpose(1, 2, 0, 3).reshape(3 * CF, -1)


def stack_in(w):
    w = jnp.pad(w, ((0, 0), (0, 0), (0, CB - w.shape[2])))
    return w.transpose(1, 0, 2).reshape(w.shape[1], 9 * CB)


def adjoint_taps(w):
    return jnp.flip(w, 0).transpose(0, 2, 1)


def by_rows(x):
    x = x.transpose(1, 0, 2)
    return jnp.pad(x, ((0, 0), (0, CF - x.shape[1]), (0, 0)))


def local(first_guess, background, observed, cell_mask, chan_mask, w_in, b_in, w_out):
    c, n, lon = first_guess.shape[1:]
    hid = b_in.shape[0]
    lat, lats = lax.axis_index("lat"), lax.axis_size("lat")
    tm, tms = lax.axis_index("tm"), lax.axis_size("tm")
    odd = lat % 2 == 1
    flags = jnp.stack([lat > 0, lat < lats - 1, tm < tms - 1, tm == 0, odd]).astype(F32)
    near_pairs = [p for i in range(0, lats - 1, 2) for p in ((i, i + 1), (i + 1, i))]
    far_pairs = [p for i in range(1, lats - 1, 2) for p in ((i, i + 1), (i + 1, i))]
    ahead = [(i, i + 1) for i in range(tms - 1)]
    back = [(j, i) for i, j in ahead]

    def exchange(far, near):
        return lax.ppermute(far, "lat", far_pairs), lax.ppermute(near, "lat", near_pairs)

    guess = first_guess[0]
    nxt = by_rows(lax.ppermute(guess.astype(BF16), "tm", back))
    low, high = guess[:, :2], guess[:, n - 2 :]
    far = by_rows(jnp.where(odd, high, low).astype(BF16))
    near = by_rows(jnp.where(odd, low, high).astype(BF16))
    far, near = exchange(far, near)
    state = by_rows(guess)
    xb = by_rows(guess.astype(BF16))
    obs, ground = by_rows(observed[0]), by_rows(background)
    cell = cell_mask[0]
    chan = jnp.pad(chan_mask[0].astype(F32), (0, CF - c))[:, None]
    up1, dn1 = stack_in(w_in), stack_out(w_out)
    up2, dn2 = stack_in(adjoint_taps(w_out)), stack_out(adjoint_taps(w_in))
    bias = b_in[:, None]
    S = jax.ShapeDtypeStruct
    rows_f, rows_b = S((n, CF, lon), F32), S((n, CF, lon), BF16)
    edge, mids = S((2, CF, lon), BF16), S((n - 4, CF, lon), F32)
    four, six = S((4, hid, lon), BF16), S((n - 2, hid, lon), BF16)
    unit = 2 * 9 * c * hid * lon

    def call(body, name, count, outs, scratch, rows):
        return pl.pallas_call(
            body,
            out_shape=outs,
            in_specs=([SMEM] if body in (edge_forward, edge_adjoint) else []) + [VMEM] * count,
            out_specs=(VMEM,) * len(outs),
            scratch_shapes=scratch,
            compiler_params=pltpu.CompilerParams(vmem_limit_bytes=16 * 2**20),
            cost_estimate=pl.CostEstimate(flops=rows * unit, bytes_accessed=4 * 2**20, transcendentals=0),
            name=name,
        )

    def scratch(x_rows, h_rows):
        return [pltpu.VMEM((x_rows * 3 * CB, lon), BF16), pltpu.VMEM((h_rows * hid, lon), BF16)]

    fwd_in = call(inner_forward, "inner_forward", 5, (mids, four, six), scratch(n, n - 2), 10)
    fwd_out = call(edge_forward, "edge_forward", 13, (rows_b, rows_b, edge, edge, four, rows_f),
                   scratch(8, 8) + [pltpu.VMEM((CF, lon), F32)], 8)
    adj_in = call(inner_adjoint, "inner_adjoint", 4, (mids, four), scratch(n, n - 2), 10)
    adj_out = call(edge_adjoint, "edge_adjoint", 11, (rows_f, rows_b, edge, edge), scratch(8, 8), 8)
    for step in range(ITERS):
        mid, mid_acts, slope_in = fwd_in(xb, state, up1, bias, dn1)
        fore, lb, far, near, slope_out, acc = fwd_out(
            flags, far, near, xb, mid, mid_acts, state, obs, nxt, cell, chan, up1, bias, dn1)
        prev = lax.ppermute(fore, "tm", ahead)
        far, near = exchange(far, near)
        mid, mid_rows = adj_in(lb, slope_in, up2, dn2)
        state, xb, far, near = adj_out(
            flags, far, near, lb, mid, mid_rows, slope_out, acc, prev, ground, up2, dn2)
        if step < ITERS - 1:
            nxt = lax.ppermute(xb, "tm", back)
            far, near = exchange(far, near)
    return state[:, :c].transpose(1, 0, 2)[None]


def solution(mesh):
    return jax.shard_map(
        local,
        mesh=mesh,
        in_specs=(
            P("tm", None, "lat", None),
            P(None, "lat", None),
            P("tm", None, "lat", None),
            P("tm", "lat", None),
            P("tm", None),
            P(),
            P(),
            P(),
        ),
        out_specs=P("tm", None, "lat", None),
        check_vma=False,
    )
```

```python
import functools

import jax
import jax.numpy as jnp
from jax import lax
from jax.experimental import pallas as pl
from jax.experimental.pallas import tpu as pltpu
from jax.sharding import PartitionSpec as P


ITERS = 2
STEP = 0.25
CF = 72
CB = 80
VMEM = pl.BlockSpec(memory_space=pltpu.VMEM)
SMEM = pl.BlockSpec(memory_space=pltpu.SMEM)
F32, BF16 = jnp.float32, jnp.bfloat16


def dot(a, b):
    return jnp.dot(a, b, preferred_element_type=F32)


def shifted_sum(y):
    lon = y.shape[1]
    left = pltpu.roll(y[:CF], 1, 1)
    right = pltpu.roll(y[2 * CF :], lon - 1, 1)
    return y[CF : 2 * CF] + left + right


def place_row(dst, j, row):
    x = row.astype(F32)
    lon = x.shape[1]
    pad = jnp.zeros((CB - x.shape[0], lon), F32)
    for i, v in enumerate((pltpu.roll(x, 1, 1), x, pltpu.roll(x, lon - 1, 1))):
        dst[pl.ds((3 * j + i) * CB, CB), :] = jnp.concatenate([v, pad], axis=0).astype(BF16)


def window(ref, j, unit):
    return ref[pl.ds(j * unit, 3 * unit), :]


def halos(flags, far, near, i):
    odd = flags[4] > 0.5
    a, b = far[i].astype(F32), near[i].astype(F32)
    return jnp.where(odd, b, a), jnp.where(odd, a, b)


def send_edges(flags, rows, far_out, near_out):
    odd = flags[4] > 0.5
    for i in range(2):
        low, high = rows[i], rows[2 + i]
        far_out[i] = jnp.where(odd, high, low).astype(BF16)
        near_out[i] = jnp.where(odd, low, high).astype(BF16)


def inner_forward(own, state, wup, bias, wdn, fore_out, acts_out, slope_out, xs, acts):
    n, hid = own.shape[0], bias.shape[0]

    def up(j):
        z = dot(wup[...], window(xs, j - 1, 3 * CB)) + wide(bias, own.shape[2])
        s = jax.nn.sigmoid(z)
        act = z * s
        slope_out[j - 1] = (s + act * (1.0 - s)).astype(BF16)
        act = act.astype(BF16)
        acts[pl.ds((j - 1) * hid, hid), :] = act
        if j in (1, 2):
            acts_out[j - 1] = act
        if j in (n - 3, n - 2):
            acts_out[j - n + 5] = act

    def down(r):
        fore_out[r - 2] = state[r] + shifted_sum(dot(wdn[...], window(acts, r - 2, hid)))

    place_row(xs, 0, own[0])
    place_row(xs, 1, own[1])
    for j in range(1, n - 1):
        place_row(xs, j + 1, own[j + 1])
        up(j)
        if j >= 3:
            down(j - 1)


def column(row, size):
    m = row.shape[1]
    at = lax.broadcasted_iota(jnp.int32, (size, m), 0) == lax.broadcasted_iota(jnp.int32, (size, m), 1)
    return jnp.sum(jnp.where(at, row, 0.0), axis=1, keepdims=True)


def padded(v, size):
    return jnp.concatenate([v, jnp.zeros((size - v.shape[0], v.shape[1]), F32)], axis=0)


def prepare(flags, guess, b_row, chan_row, state_out, xb_out, far_out, near_out, bias_out, chan_out):
    n = guess.shape[1]
    rows = {}
    for r in (0, 1, n - 2, n - 1, *range(2, n - 2)):
        rows[r] = padded(guess[:, r, :], CF)
        state_out[r] = rows[r]
        xb_out[r] = rows[r].astype(BF16)
    send_edges(flags, [rows[r] for r in (0, 1, n - 2, n - 1)], far_out, near_out)
    bias_out[...] = jnp.broadcast_to(column(b_row[...], bias_out.shape[0]), bias_out.shape)
    chan_out[...] = jnp.broadcast_to(column(chan_row[...].astype(F32), CF), chan_out.shape)


def stack_in(taps, out):
    width = out.shape[1]
    whole = padded(jnp.concatenate([padded(t, CB) for t in taps], axis=0), -(-width // 128) * 128)
    for at in range(0, width, 128):
        size = min(128, width - at)
        out[:, at : at + size] = whole[at : at + 128].T[:, :size].astype(BF16)


def stack_out(taps, out):
    hid = taps[0].shape[1]
    for dr in range(3):
        rows = jnp.concatenate([padded(t, CF) for t in taps[3 * dr : 3 * dr + 3]], axis=0)
        out[:, dr * hid : (dr + 1) * hid] = rows.astype(BF16)


def prepare_forward(w_in, w_out, field, up_out, down_out, rows_out):
    stack_in([w_in[t].astype(F32).T for t in range(9)], up_out)
    stack_out([w_out[t].astype(F32) for t in range(9)], down_out)
    for r in range(field.shape[1]):
        rows_out[r] = padded(field[:, r, :], CF)


def prepare_adjoint(w_in, w_out, field, up_out, down_out, rows_out):
    stack_in([w_out[8 - t].astype(F32) for t in range(9)], up_out)
    stack_out([w_in[8 - t].astype(F32).T for t in range(9)], down_out)
    for r in range(field.shape[1]):
        rows_out[r] = padded(field[:, r, :], CF)


def wide(bias, lon):
    return jnp.concatenate([bias[...]] * (lon // bias.shape[1]), axis=1)


def edge_forward(flags, far, near, own, inner, inner_acts, state, wup, bias, wdn,
                 fore_out, edges_out, slope_out, xs, acts):
    n, hid = own.shape[0], bias.shape[0]
    has_low, has_high = flags[0], flags[1]
    for i in range(2):
        below, above = halos(flags, far, near, i)
        place_row(xs, i, below)
        place_row(xs, 2 + i, own[i])
        place_row(xs, 4 + i, own[n - 2 + i])
        place_row(xs, 6 + i, above)
        acts[pl.ds((2 + i) * hid, hid), :] = inner_acts[i]
        acts[pl.ds((4 + i) * hid, hid), :] = inner_acts[2 + i]

    def up(x_at, act_at, slope_at, inside):
        z = dot(wup[...], window(xs, x_at, 3 * CB)) + wide(bias, own.shape[2])
        s = jax.nn.sigmoid(z)
        act = z * s
        slope = s + act * (1.0 - s)
        if inside is not None:
            act, slope = act * inside, slope * inside
        acts[pl.ds(act_at * hid, hid), :] = act.astype(BF16)
        slope_out[slope_at] = slope.astype(BF16)

    up(0, 0, 0, has_low)
    up(1, 1, 1, None)
    up(4, 6, 2, None)
    up(5, 7, 3, has_high)
    for i, (r, at) in enumerate(((0, 0), (1, 1), (n - 2, 4), (n - 1, 5))):
        fore = state[r] + shifted_sum(dot(wdn[...], window(acts, at, hid)))
        edges_out[i] = fore
        fore_out[r] = fore.astype(BF16)
    for r in range(2, n - 2):
        fore_out[r] = inner[r - 2].astype(BF16)


def misfit(flags, inner, outer, state, obs, nxt, cell, chan, lb_out, far_out, near_out, acc_out):
    n = state.shape[0]
    has_next = flags[2]

    def finish(r, fore):
        st = state[r]
        w = chan[...] * cell[pl.ds(r, 1), :].astype(F32)
        lam = w * (fore - obs[r]) - has_next * (nxt[r].astype(F32) - fore)
        lb_out[r] = lam.astype(BF16)
        acc_out[r] = st - STEP * (st + lam)
        return lam

    edges = [finish(r, outer[i]) for i, r in enumerate((0, 1, n - 2, n - 1))]
    send_edges(flags, edges, far_out, near_out)
    for r in range(2, n - 2):
        finish(r, inner[r - 2])


def inner_adjoint(own, slope, wup, wdn, grad_out, rows_out, xs, grads):
    n, hid = own.shape[0], slope.shape[1]

    def up(j):
        g = (dot(wup[...], window(xs, j - 1, 3 * CB)) * slope[j - 1].astype(F32)).astype(BF16)
        grads[pl.ds((j - 1) * hid, hid), :] = g
        if j in (1, 2):
            rows_out[j - 1] = g
        if j in (n - 3, n - 2):
            rows_out[j - n + 5] = g

    def down(r):
        grad_out[r - 2] = shifted_sum(dot(wdn[...], window(grads, r - 2, hid)))

    place_row(xs, 0, own[0])
    place_row(xs, 1, own[1])
    for j in range(1, n - 1):
        place_row(xs, j + 1, own[j + 1])
        up(j)
        if j >= 3:
            down(j - 1)


def edge_adjoint(last, flags, far, near, own, inner, inner_rows, slope, acc, prev, ground, wup, wdn, *refs):
    outs, (xs, grads) = refs[:-2], refs[-2:]
    n, hid = own.shape[0], slope.shape[1]
    first = flags[3] > 0.5
    for i in range(2):
        below, above = halos(flags, far, near, i)
        place_row(xs, i, below)
        place_row(xs, 2 + i, own[i])
        place_row(xs, 4 + i, own[n - 2 + i])
        place_row(xs, 6 + i, above)
        grads[pl.ds((2 + i) * hid, hid), :] = inner_rows[i]
        grads[pl.ds((4 + i) * hid, hid), :] = inner_rows[2 + i]

    def up(x_at, at, slope_at):
        g = dot(wup[...], window(xs, x_at, 3 * CB)) * slope[slope_at].astype(F32)
        grads[pl.ds(at * hid, hid), :] = g.astype(BF16)

    def finish(r, grad):
        earlier = jnp.where(first, ground[r], prev[r].astype(F32))
        st = acc[r] + STEP * (earlier - grad)
        if last:
            outs[0][:, r, :] = st[: outs[0].shape[0]]
        else:
            outs[0][r] = st
            outs[1][r] = st.astype(BF16)
        return st

    up(0, 0, 0)
    up(1, 1, 1)
    up(4, 6, 2)
    up(5, 7, 3)
    edges = [
        finish(r, shifted_sum(dot(wdn[...], window(grads, at, hid))))
        for r, at in ((0, 0), (1, 1), (n - 2, 4), (n - 1, 5))
    ]
    if not last:
        send_edges(flags, edges, outs[2], outs[3])
    for r in range(2, n - 2):
        finish(r, inner[r - 2])


def local(first_guess, background, observed, cell_mask, chan_mask, w_in, b_in, w_out):
    c, n, lon = first_guess.shape[1:]
    hid = b_in.shape[0]
    lat, lats = lax.axis_index("lat"), lax.axis_size("lat")
    tm, tms = lax.axis_index("tm"), lax.axis_size("tm")
    odd = lat % 2 == 1
    flags = jnp.stack([lat > 0, lat < lats - 1, tm < tms - 1, tm == 0, odd]).astype(F32)
    near_pairs = [p for i in range(0, lats - 1, 2) for p in ((i, i + 1), (i + 1, i))]
    far_pairs = [p for i in range(1, lats - 1, 2) for p in ((i, i + 1), (i + 1, i))]
    ahead = [(i, i + 1) for i in range(tms - 1)]
    back = [(j, i) for i, j in ahead]

    def exchange(far, near):
        far = lax.ppermute(far, "lat", far_pairs)
        near = lax.ppermute(near, "lat", near_pairs)
        return far, near

    def shift(x, pairs):
        return lax.ppermute(x, "tm", pairs)

    cell = cell_mask[0]
    S = jax.ShapeDtypeStruct
    rows_f, rows_b = S((n, CF, lon), F32), S((n, CF, lon), BF16)
    edge, mids = S((2, CF, lon), BF16), S((n - 4, CF, lon), F32)
    four, six = S((4, hid, lon), BF16), S((n - 2, hid, lon), BF16)
    unit = 2 * 9 * c * hid * lon

    def call(body, count, outs, scratch, rows, flagged=True):
        return pl.pallas_call(
            body,
            out_shape=outs,
            in_specs=[SMEM] * flagged + [VMEM] * count,
            out_specs=(VMEM,) * len(outs),
            scratch_shapes=scratch,
            compiler_params=pltpu.CompilerParams(vmem_limit_bytes=16 * 2**20),
            cost_estimate=pl.CostEstimate(flops=rows * unit, bytes_accessed=4 * 2**20, transcendentals=0),
        )

    def scratch(x_rows, h_rows):
        return [pltpu.VMEM((x_rows * 3 * CB, lon), BF16), pltpu.VMEM((h_rows * hid, lon), BF16)]

    ups, downs = S((hid, 9 * CB), BF16), S((3 * CF, 3 * hid), BF16)
    prep = call(prepare, 3, (rows_f, rows_b, edge, edge, S((hid, 128), F32), S((CF, lon), F32)), [], 0)
    prep_fwd = call(prepare_forward, 3, (ups, downs, rows_f), [], 4, False)
    prep_adj = call(prepare_adjoint, 3, (ups, downs, rows_f), [], 4, False)
    fwd_in = call(inner_forward, 5, (mids, four, six), scratch(n, n - 2), 10, False)
    fwd_out = call(edge_forward, 9, (rows_b, mids, four), scratch(8, 8), 8)
    fit = call(misfit, 7, (rows_b, edge, edge, rows_f), [], 0)
    adj_in = call(inner_adjoint, 4, (mids, four), scratch(n, n - 2), 10, False)
    adj_out = call(functools.partial(edge_adjoint, False), 11, (rows_f, rows_b, edge, edge), scratch(8, 8), 8)
    adj_end = call(functools.partial(edge_adjoint, True), 11, (S((c, n, lon), F32),), scratch(8, 8), 8)
    state, xb, far, near, bias, chan = prep(flags, first_guess[0], b_in[None], chan_mask)
    for step in range(ITERS):
        far, near = exchange(far, near)
        nxt = shift(xb, back)
        if step == 0:
            up1, dn1, obs = prep_fwd(w_in, w_out, observed[0])
        mid, mid_acts, slope_in = fwd_in(xb, state, up1, bias, dn1)
        fore, outer, slope_out = fwd_out(flags, far, near, xb, mid, mid_acts, state, up1, bias, dn1)
        prev = shift(fore, ahead)
        lb, far, near, acc = fit(flags, mid, outer, state, obs, nxt, cell, chan)
        far, near = exchange(far, near)
        if step == 0:
            up2, dn2, ground = prep_adj(w_in, w_out, background)
        mid, mid_rows = adj_in(lb, slope_in, up2, dn2)
        tail = (flags, far, near, lb, mid, mid_rows, slope_out, acc, prev, ground, up2, dn2)
        if step < ITERS - 1:
            state, xb, far, near = adj_out(*tail)
        else:
            (analysis,) = adj_end(*tail)
    return analysis[None]


def solution(mesh):
    return jax.shard_map(
        local,
        mesh=mesh,
        in_specs=(
            P("tm", None, "lat", None),
            P(None, "lat", None),
            P("tm", None, "lat", None),
            P("tm", "lat", None),
            P("tm", None),
            P(),
            P(),
            P(),
        ),
        out_specs=P("tm", None, "lat", None),
        check_vma=False,
    )
```

```python
import functools

import jax
import jax.numpy as jnp
from jax import lax
from jax.experimental import pallas as pl
from jax.experimental.pallas import tpu as pltpu
from jax.sharding import PartitionSpec as P


ITERS = 2
STEP = 0.25
CF = 72
CB = 80
VMEM = pl.BlockSpec(memory_space=pltpu.VMEM)
SMEM = pl.BlockSpec(memory_space=pltpu.SMEM)
F32, BF16 = jnp.float32, jnp.bfloat16


def dot(a, b):
    return jnp.dot(a, b, preferred_element_type=F32)


def shifted_sum(y):
    lon = y.shape[1]
    left = pltpu.roll(y[:CF], 1, 1)
    right = pltpu.roll(y[2 * CF :], lon - 1, 1)
    return y[CF : 2 * CF] + left + right


def place_row(dst, j, row):
    x = row.astype(F32)
    lon = x.shape[1]
    pad = jnp.zeros((CB - x.shape[0], lon), F32)
    for i, v in enumerate((pltpu.roll(x, 1, 1), x, pltpu.roll(x, lon - 1, 1))):
        dst[pl.ds((3 * j + i) * CB, CB), :] = jnp.concatenate([v, pad], axis=0).astype(BF16)


def window(ref, j, unit):
    return ref[pl.ds(j * unit, 3 * unit), :]


def own_row(edge, inner, r):
    n = edge.shape[0] + inner.shape[0]
    return edge[r] if r < 2 else inner[r - 2] if r < n - 2 else edge[r - n + 4]


def edge_rows(n):
    return 0, 1, n - 2, n - 1


def halos(flags, far, near, i):
    odd = flags[4] > 0.5
    a, b = far[i].astype(F32), near[i].astype(F32)
    return jnp.where(odd, b, a), jnp.where(odd, a, b)


def send_edges(flags, rows, far_out, near_out):
    odd = flags[4] > 0.5
    for i in range(2):
        low, high = rows[i], rows[2 + i]
        far_out[i] = jnp.where(odd, high, low).astype(BF16)
        near_out[i] = jnp.where(odd, low, high).astype(BF16)


def column(row, size):
    m = row.shape[1]
    at = lax.broadcasted_iota(jnp.int32, (size, m), 0) == lax.broadcasted_iota(jnp.int32, (size, m), 1)
    return jnp.sum(jnp.where(at, row, 0.0), axis=1, keepdims=True)


def padded(v, size):
    return jnp.concatenate([v, jnp.zeros((size - v.shape[0], v.shape[1]), F32)], axis=0)


def stack_in(taps, out):
    width = out.shape[1]
    whole = padded(jnp.concatenate([padded(t, CB) for t in taps], axis=0), -(-width // 128) * 128)
    for at in range(0, width, 128):
        size = min(128, width - at)
        out[:, at : at + size] = whole[at : at + 128].T[:, :size].astype(BF16)


def stack_out(taps, out):
    hid = taps[0].shape[1]
    for dr in range(3):
        rows = jnp.concatenate([padded(t, CF) for t in taps[3 * dr : 3 * dr + 3]], axis=0)
        out[:, dr * hid : (dr + 1) * hid] = rows.astype(BF16)


def prepare(flags, guess, state_e, state_i, xb_out, far_out, near_out):
    n = guess.shape[1]
    rows = [padded(guess[:, r, :], CF) for r in edge_rows(n)]
    send_edges(flags, rows, far_out, near_out)
    for i, row in enumerate(rows):
        state_e[i] = row
        xb_out[i] = row.astype(BF16)
    for i in range(n - 4):
        row = padded(guess[:, i + 2, :], CF)
        state_i[i] = row
        xb_out[4 + i] = row.astype(BF16)


def prepare_forward(w_in, w_out, field, b_row, chan_row, up_out, down_out, rows_out, bias_out, chan_out):
    stack_in([w_in[t].astype(F32) for t in range(9)], up_out)
    stack_out([w_out[t].astype(F32) for t in range(9)], down_out)
    for r in range(field.shape[1]):
        rows_out[r] = padded(field[:, r, :], CF)
    bias_out[...] = jnp.broadcast_to(column(b_row[...], bias_out.shape[0]), bias_out.shape)
    chan_out[...] = jnp.broadcast_to(column(chan_row[...].astype(F32), CF), chan_out.shape)


def prepare_adjoint(w_in, w_out, field, up_out, down_out, rows_out):
    stack_in([w_out[8 - t].astype(F32) for t in range(9)], up_out)
    stack_out([w_in[8 - t].astype(F32) for t in range(9)], down_out)
    for r in range(field.shape[1]):
        rows_out[r] = padded(field[:, r, :], CF)


def wide(bias, lon):
    return jnp.concatenate([bias[...]] * (lon // bias.shape[1]), axis=1)


def activate(wup, bias, xs, at):
    z = dot(wup[...], window(xs, at, 3 * CB)) + wide(bias, xs.shape[1])
    s = jax.nn.sigmoid(z)
    act = z * s
    return act, s + act * (1.0 - s)


def inner_forward(joined, own_e, own_i, state, wup, bias, wdn, fore_out, send_out, acts_out, slope_out, xs, acts):
    if joined:
        own_e, own_i = own_e.at[:4], own_e.at[4:]
    n, hid = own_e.shape[0] + own_i.shape[0], bias.shape[0]

    def up(j):
        act, slope = activate(wup, bias, xs, j - 1)
        slope_out[j - 1] = slope.astype(BF16)
        act = act.astype(BF16)
        acts[pl.ds((j - 1) * hid, hid), :] = act
        if j in (1, 2):
            acts_out[j - 1] = act
        if j in (n - 3, n - 2):
            acts_out[j - n + 5] = act

    def down(i):
        fore = state[i] + shifted_sum(dot(wdn[...], window(acts, i, hid)))
        fore_out[i] = fore
        send_out[i] = fore.astype(BF16)

    for j in range(2):
        place_row(xs, j, own_row(own_e, own_i, j))
    for j in range(1, n - 1):
        place_row(xs, j + 1, own_row(own_e, own_i, j + 1))
        up(j)
        if j >= 3:
            down(j - 3)


def misfit(has_next, st, fore, obs, nxt, cell, chan):
    lam = chan[...] * cell.astype(F32) * (fore - obs) - has_next * (nxt.astype(F32) - fore)
    return lam, st - STEP * (st + lam)


def inner_misfit(flags, fore, state, obs, nxt, cell, chan, lb_out, acc_out):
    skip = nxt.shape[0] - state.shape[0]
    for i in range(state.shape[0]):
        lam, acc = misfit(flags[2], state[i], fore[i], obs[i + 2], nxt[i + skip], cell[pl.ds(i + 2, 1), :], chan)
        lb_out[i] = lam.astype(BF16)
        acc_out[i] = acc


def place_edges(flags, far, near, own, inner, xs, hidden, hid):
    for i in range(2):
        below, above = halos(flags, far, near, i)
        place_row(xs, i, below)
        place_row(xs, 2 + i, own[i])
        place_row(xs, 4 + i, own[2 + i])
        place_row(xs, 6 + i, above)
        hidden[pl.ds((2 + i) * hid, hid), :] = inner[i]
        hidden[pl.ds((4 + i) * hid, hid), :] = inner[2 + i]


def edge_forward(flags, far, near, own, inner_acts, state, obs, nxt, cell, chan, wup, bias, wdn,
                 send_out, lb_out, far_out, near_out, slope_out, acc_out, xs, acts):
    n, hid = obs.shape[0], bias.shape[0]
    place_edges(flags, far, near, own, inner_acts, xs, acts, hid)
    for i, (x_at, act_at, inside) in enumerate(
        ((0, 0, flags[0]), (1, 1, None), (4, 6, None), (5, 7, flags[1]))
    ):
        act, slope = activate(wup, bias, xs, x_at)
        if inside is not None:
            act, slope = act * inside, slope * inside
        acts[pl.ds(act_at * hid, hid), :] = act.astype(BF16)
        slope_out[i] = slope.astype(BF16)
    lams = []
    for i, (r, at) in enumerate(zip(edge_rows(n), (0, 1, 4, 5))):
        fore = state[i] + shifted_sum(dot(wdn[...], window(acts, at, hid)))
        send_out[i] = fore.astype(BF16)
        lam, acc = misfit(flags[2], state[i], fore, obs[r], nxt[i], cell[pl.ds(r, 1), :], chan)
        lb_out[i] = lam.astype(BF16)
        acc_out[i] = acc
        lams.append(lam)
    send_edges(flags, lams, far_out, near_out)


def descend(flags, acc, prev, ground, grad):
    earlier = jnp.where(flags[3] > 0.5, ground, prev.astype(F32))
    return acc + STEP * (earlier - grad)


def inner_adjoint(flags, own_e, own_i, slope, acc, prev, ground, wup, wdn, state_out, xb_out, rows_out, xs, grads):
    n, hid = own_e.shape[0] + own_i.shape[0], slope.shape[1]

    def up(j):
        g = (dot(wup[...], window(xs, j - 1, 3 * CB)) * slope[j - 1].astype(F32)).astype(BF16)
        grads[pl.ds((j - 1) * hid, hid), :] = g
        if j in (1, 2):
            rows_out[j - 1] = g
        if j in (n - 3, n - 2):
            rows_out[j - n + 5] = g

    def down(i):
        grad = shifted_sum(dot(wdn[...], window(grads, i, hid)))
        st = descend(flags, acc[i], prev[i], ground[i + 2], grad)
        state_out[i] = st
        xb_out[i] = st.astype(BF16)

    for j in range(2):
        place_row(xs, j, own_row(own_e, own_i, j))
    for j in range(1, n - 1):
        place_row(xs, j + 1, own_row(own_e, own_i, j + 1))
        up(j)
        if j >= 3:
            down(j - 3)


def edge_states(flags, far, near, own, inner_rows, slope, acc, prev, ground, wup, wdn, xs, grads):
    n, hid = ground.shape[0], slope.shape[1]
    place_edges(flags, far, near, own, inner_rows, xs, grads, hid)
    for i, (x_at, at) in enumerate(((0, 0), (1, 1), (4, 6), (5, 7))):
        g = dot(wup[...], window(xs, x_at, 3 * CB)) * slope[i].astype(F32)
        grads[pl.ds(at * hid, hid), :] = g.astype(BF16)
    return [
        descend(flags, acc[i], prev[i], ground[r], shifted_sum(dot(wdn[...], window(grads, at, hid))))
        for i, (r, at) in enumerate(zip(edge_rows(n), (0, 1, 4, 5)))
    ]


def edge_adjoint(*refs):
    (state_out, xb_out, far_out, near_out), scratch = refs[11:15], refs[15:]
    rows = edge_states(*refs[:11], *scratch)
    send_edges(refs[0], rows, far_out, near_out)
    for i, row in enumerate(rows):
        state_out[i] = row
        xb_out[i] = row.astype(BF16)


def last_adjoint(*refs):
    inner, out, scratch = refs[11], refs[12], refs[13:]
    c, n = out.shape[:2]
    for r in range(2, n - 2):
        out[:, r, :] = inner[r - 2][:c]
    for r, row in zip(edge_rows(n), edge_states(*refs[:11], *scratch)):
        out[:, r, :] = row[:c]


def local(first_guess, background, observed, cell_mask, chan_mask, w_in, b_in, w_out):
    c, n, lon = first_guess.shape[1:]
    hid = b_in.shape[0]
    lat, lats = lax.axis_index("lat"), lax.axis_size("lat")
    tm, tms = lax.axis_index("tm"), lax.axis_size("tm")
    odd = lat % 2 == 1
    flags = jnp.stack([lat > 0, lat < lats - 1, tm < tms - 1, tm == 0, odd]).astype(F32)
    near_pairs = [p for i in range(0, lats - 1, 2) for p in ((i, i + 1), (i + 1, i))]
    far_pairs = [p for i in range(1, lats - 1, 2) for p in ((i, i + 1), (i + 1, i))]
    ahead = [(i, i + 1) for i in range(tms - 1)]
    back = [(j, i) for i, j in ahead]

    def exchange(far, near):
        far = lax.ppermute(far, "lat", far_pairs)
        near = lax.ppermute(near, "lat", near_pairs)
        return far, near

    def shift(x, pairs):
        return lax.ppermute(x, "tm", pairs)

    cell = cell_mask[0]
    w_in = w_in.transpose(0, 2, 1)
    S = jax.ShapeDtypeStruct
    rows = S((n, CF, lon), F32)
    edge, four_f, four_b = S((2, CF, lon), BF16), S((4, CF, lon), F32), S((4, CF, lon), BF16)
    mid_f, mid_b = S((n - 4, CF, lon), F32), S((n - 4, CF, lon), BF16)
    four_h, six_h = S((4, hid, lon), BF16), S((n - 2, hid, lon), BF16)
    ups, downs = S((hid, 9 * CB), BF16), S((3 * CF, 3 * hid), BF16)
    bias_s, chan_s = S((hid, 128), F32), S((CF, lon), F32)
    unit = 2 * 9 * c * hid * lon

    def call(body, count, outs, held=0, work=0, flagged=True):
        return pl.pallas_call(
            body,
            out_shape=outs,
            in_specs=[SMEM] * flagged + [VMEM] * count,
            out_specs=(VMEM,) * len(outs),
            scratch_shapes=[pltpu.VMEM((8 * 3 * CB, lon), BF16), pltpu.VMEM((held * hid, lon), BF16)] if held else [],
            compiler_params=pltpu.CompilerParams(vmem_limit_bytes=16 * 2**20),
            cost_estimate=pl.CostEstimate(flops=work * unit, bytes_accessed=4 * 2**20, transcendentals=0),
        )

    state_e, state_i, xb_e, far, near = call(prepare, 1, (four_f, mid_f, S((n, CF, lon), BF16), edge, edge))(
        flags, first_guess[0])
    xb_i = nxt_i = None
    for step in range(ITERS):
        joined = xb_i is None
        far, near = exchange(far, near)
        nxt_e = shift(xb_e, back)
        if joined:
            nxt_i = nxt_e
            up1, dn1, obs, bias, chan = call(
                prepare_forward, 5, (ups, downs, rows, bias_s, chan_s), work=4, flagged=False
            )(w_in, w_out, observed[0], b_in[None], chan_mask)
        fore_i, send, mid_acts, slope_i = call(
            functools.partial(inner_forward, joined), 6, (mid_f, mid_b, four_h, six_h), n - 2, 10, False,
        )(xb_e, xb_e if joined else xb_i, state_i, up1, bias, dn1)
        prev_i = shift(send, ahead)
        send, lb_e, far, near, slope_e, acc_e = call(
            edge_forward, 12, (four_b, four_b, edge, edge, four_h, four_f), 8, 8
        )(flags, far, near, xb_e, mid_acts, state_e, obs, nxt_e, cell, chan, up1, bias, dn1)
        far, near = exchange(far, near)
        prev_e = shift(send, ahead)
        lb_i, acc_i = call(inner_misfit, 6, (mid_b, mid_f))(flags, fore_i, state_i, obs, nxt_i, cell, chan)
        if step == 0:
            up2, dn2, ground = call(
                prepare_adjoint, 3, (ups, downs, rows), work=4, flagged=False
            )(w_in, w_out, background)
        state_i, xb_i, mid_rows = call(
            inner_adjoint, 8, (mid_f, mid_b, four_h), n - 2, 10
        )(flags, lb_e, lb_i, slope_i, acc_i, prev_i, ground, up2, dn2)
        tail = (flags, far, near, lb_e, mid_rows, slope_e, acc_e, prev_e, ground, up2, dn2)
        if step < ITERS - 1:
            nxt_i = shift(xb_i, back)
            state_e, xb_e, far, near = call(edge_adjoint, 10, (four_f, four_b, edge, edge), 8, 8)(*tail)
        else:
            (analysis,) = call(last_adjoint, 11, (S((c, n, lon), F32),), 8, 8)(*tail, state_i)
    return analysis[None]


def solution(mesh):
    return jax.shard_map(
        local,
        mesh=mesh,
        in_specs=(
            P("tm", None, "lat", None),
            P(None, "lat", None),
            P("tm", None, "lat", None),
            P("tm", "lat", None),
            P("tm", None),
            P(),
            P(),
            P(),
        ),
        out_specs=P("tm", None, "lat", None),
        check_vma=False,
    )
```

```python
import jax
import jax.numpy as jnp
from jax import lax
from jax.experimental import pallas as pl
from jax.experimental.pallas import tpu as pltpu
from jax.sharding import PartitionSpec as P


ITERS = 2
STEP = 0.25
CF = 72
CB = 80
ROW = 256
VMEM = pl.BlockSpec(memory_space=pltpu.VMEM)
SMEM = pl.BlockSpec(memory_space=pltpu.SMEM)
F32, BF16 = jnp.float32, jnp.bfloat16


def dot(a, b):
    return jnp.dot(a, b, preferred_element_type=F32)


def shifted_sum(y):
    lon = y.shape[1]
    left = pltpu.roll(y[:CF], 1, 1)
    right = pltpu.roll(y[2 * CF :], lon - 1, 1)
    return y[CF : 2 * CF] + left + right


def place_row(dst, j, row):
    x = row.astype(F32)
    lon = x.shape[1]
    for i, v in enumerate((pltpu.roll(x, 1, 1), x, pltpu.roll(x, lon - 1, 1))):
        size = CB if i < 2 else ROW - 2 * CB
        dst[pl.ds(j * ROW + i * CB, size), :] = padded(v, size).astype(BF16)


def partial(w, rows, ref, at, unit, first):
    taps = w[:, first * unit : (first + rows) * unit]
    return dot(taps, ref[pl.ds(at * unit, rows * unit), :])


OUTER = ((0, 2), (0, 1), (2, 1), (1, 2))
INNER = ((2, 1), (1, 2), (0, 2), (0, 1))


def own_row(edge, inner, r):
    n = edge.shape[0] + inner.shape[0]
    return edge[r] if r < 2 else inner[r - 2] if r < n - 2 else edge[r - n + 4]


def edge_rows(n):
    return 0, 1, n - 2, n - 1


def halos(flags, far, near, i):
    odd = flags[4] > 0.5
    a, b = far[i].astype(F32), near[i].astype(F32)
    return jnp.where(odd, b, a), jnp.where(odd, a, b)


def send_edges(flags, rows, far_out, near_out):
    odd = flags[4] > 0.5
    for i in range(2):
        low, high = rows[i], rows[2 + i]
        far_out[i] = jnp.where(odd, high, low).astype(BF16)
        near_out[i] = jnp.where(odd, low, high).astype(BF16)


def column(row, size):
    m = row.shape[1]
    at = lax.broadcasted_iota(jnp.int32, (size, m), 0) == lax.broadcasted_iota(jnp.int32, (size, m), 1)
    return jnp.sum(jnp.where(at, row, 0.0), axis=1, keepdims=True)


def padded(v, size):
    return jnp.concatenate([v, jnp.zeros((size - v.shape[0], v.shape[1]), F32)], axis=0)


def stack_in(taps, out):
    groups = [
        padded(jnp.concatenate([padded(t, CB) for t in taps[3 * dr : 3 * dr + 3]], axis=0), ROW) for dr in range(3)
    ]
    whole = jnp.concatenate(groups, axis=0)
    for at in range(0, 3 * ROW, 128):
        out[:, at : at + 128] = whole[at : at + 128].T.astype(BF16)


def stack_out(taps, out):
    hid = taps[0].shape[1]
    for dr in range(3):
        rows = jnp.concatenate([padded(t, CF) for t in taps[3 * dr : 3 * dr + 3]], axis=0)
        out[:, dr * hid : (dr + 1) * hid] = rows.astype(BF16)


def prepare(flags, guess, state_e, state_i, xb_out, far_out, near_out):
    n = guess.shape[1]
    rows = [padded(guess[:, r, :], CF) for r in edge_rows(n)]
    send_edges(flags, rows, far_out, near_out)
    for i, row in enumerate(rows):
        state_e[i] = row
        xb_out[i] = row.astype(BF16)
    for i in range(n - 4):
        row = padded(guess[:, i + 2, :], CF)
        state_i[i] = row
        xb_out[4 + i] = row.astype(BF16)


def prepare_forward(w_in, w_out, field, b_row, chan_row, up_out, down_out, rows_out, bias_out, chan_out):
    stack_in([w_in[t].astype(F32) for t in range(9)], up_out)
    stack_out([w_out[t].astype(F32) for t in range(9)], down_out)
    for r in range(field.shape[1]):
        rows_out[r] = padded(field[:, r, :], CF)
    bias_out[...] = jnp.broadcast_to(column(b_row[...], bias_out.shape[0]), bias_out.shape)
    chan_out[...] = jnp.broadcast_to(column(chan_row[...].astype(F32), CF), chan_out.shape)


def prepare_adjoint(w_in, w_out, field, up_out, down_out, rows_out):
    stack_in([w_out[8 - t].astype(F32) for t in range(9)], up_out)
    stack_out([w_in[8 - t].astype(F32) for t in range(9)], down_out)
    for r in range(field.shape[1]):
        rows_out[r] = padded(field[:, r, :], CF)


def wide(bias, lon):
    return jnp.concatenate([bias[...]] * (lon // bias.shape[1]), axis=1)


def activate(z):
    s = jax.nn.sigmoid(z)
    act = z * s
    return act, s + act * (1.0 - s)


def edge_partials(wup, wdn, xs, n, hidden, hid, up_out, down_out):
    for i, (first, count) in enumerate(INNER):
        up_out[i] = partial(wup, count, xs, 0 if i < 2 else n - count, ROW, first)
    for i, (first, count) in enumerate(INNER):
        down_out[i] = shifted_sum(partial(wdn, count, hidden, 0 if i < 2 else n - 2 - count, hid, first))


def inner_forward(own_e, own_i, state, wup, bias, wdn, fore_out, send_out, slope_out, up_out, down_out, xs, acts):
    if own_i is None:
        own_e, own_i = own_e.at[:4], own_e.at[4:]
    n, hid = own_e.shape[0] + own_i.shape[0], bias.shape[0]
    wide_bias = wide(bias, xs.shape[1])

    def up(j):
        act, slope = activate(partial(wup, 3, xs, j - 1, ROW, 0) + wide_bias)
        slope_out[j - 1] = slope.astype(BF16)
        acts[pl.ds((j - 1) * hid, hid), :] = act.astype(BF16)

    def down(i):
        fore = state[i] + shifted_sum(partial(wdn, 3, acts, i, hid, 0))
        fore_out[i] = fore
        send_out[i] = fore.astype(BF16)

    for j in range(2):
        place_row(xs, j, own_row(own_e, own_i, j))
    for j in range(1, n - 1):
        place_row(xs, j + 1, own_row(own_e, own_i, j + 1))
        up(j)
        if j >= 3:
            down(j - 3)
    edge_partials(wup, wdn, xs, n, acts, hid, up_out, down_out)


def first_forward(own, *refs):
    inner_forward(own, None, *refs)


def misfit(has_next, st, fore, obs, nxt, cell, chan):
    lam = chan[...] * cell.astype(F32) * (fore - obs) - has_next * (nxt.astype(F32) - fore)
    return lam, st - STEP * (st + lam)


def inner_misfit(flags, fore, state, obs, nxt, cell, chan, lb_out, acc_out):
    skip = nxt.shape[0] - state.shape[0]
    for i in range(state.shape[0]):
        lam, acc = misfit(flags[2], state[i], fore[i], obs[i + 2], nxt[i + skip], cell[pl.ds(i + 2, 1), :], chan)
        lb_out[i] = lam.astype(BF16)
        acc_out[i] = acc


def place_edges(flags, far, near, xs):
    for i in range(2):
        below, above = halos(flags, far, near, i)
        place_row(xs, i, below)
        place_row(xs, 2 + i, above)


def edge_up(wup, parts, xs, i):
    first, count = OUTER[i]
    return parts[i] + partial(wup, count, xs, (0, 1, 2, 2)[i], ROW, first)


def edge_down(wdn, parts, hidden, hid, i):
    first, count = OUTER[i]
    return parts[i] + shifted_sum(partial(wdn, count, hidden, (0, 1, 2, 2)[i], hid, first))


def edge_forward(flags, far, near, up_part, down_part, state, obs, nxt, cell, chan, wup, bias, wdn,
                 send_out, lb_out, far_out, near_out, slope_out, acc_out, xs, acts):
    n, hid = obs.shape[0], bias.shape[0]
    wide_bias = wide(bias, xs.shape[1])
    place_edges(flags, far, near, xs)
    for i, inside in enumerate((flags[0], None, None, flags[1])):
        act, slope = activate(edge_up(wup, up_part, xs, i) + wide_bias)
        if inside is not None:
            act, slope = act * inside, slope * inside
        acts[pl.ds(i * hid, hid), :] = act.astype(BF16)
        slope_out[i] = slope.astype(BF16)
    lams = []
    for i, r in enumerate(edge_rows(n)):
        fore = state[i] + edge_down(wdn, down_part, acts, hid, i)
        send_out[i] = fore.astype(BF16)
        lam, acc = misfit(flags[2], state[i], fore, obs[r], nxt[i], cell[pl.ds(r, 1), :], chan)
        lb_out[i] = lam.astype(BF16)
        acc_out[i] = acc
        lams.append(lam)
    send_edges(flags, lams, far_out, near_out)


def descend(flags, acc, prev, ground, grad):
    earlier = jnp.where(flags[3] > 0.5, ground, prev.astype(F32))
    return acc + STEP * (earlier - grad)


def inner_adjoint(flags, own_e, own_i, slope, acc, prev, ground, wup, wdn,
                  state_out, xb_out, up_out, down_out, xs, grads):
    n, hid = own_e.shape[0] + own_i.shape[0], slope.shape[1]

    def up(j):
        g = partial(wup, 3, xs, j - 1, ROW, 0) * slope[j - 1].astype(F32)
        grads[pl.ds((j - 1) * hid, hid), :] = g.astype(BF16)

    def down(i):
        grad = shifted_sum(partial(wdn, 3, grads, i, hid, 0))
        st = descend(flags, acc[i], prev[i], ground[i + 2], grad)
        state_out[i] = st
        xb_out[i] = st.astype(BF16)

    for j in range(2):
        place_row(xs, j, own_row(own_e, own_i, j))
    for j in range(1, n - 1):
        place_row(xs, j + 1, own_row(own_e, own_i, j + 1))
        up(j)
        if j >= 3:
            down(j - 3)
    edge_partials(wup, wdn, xs, n, grads, hid, up_out, down_out)


def edge_states(flags, far, near, up_part, down_part, slope, acc, prev, ground, wup, wdn, xs, grads):
    n, hid = ground.shape[0], slope.shape[1]
    place_edges(flags, far, near, xs)
    for i in range(4):
        g = edge_up(wup, up_part, xs, i) * slope[i].astype(F32)
        grads[pl.ds(i * hid, hid), :] = g.astype(BF16)
    return [
        descend(flags, acc[i], prev[i], ground[r], edge_down(wdn, down_part, grads, hid, i))
        for i, r in enumerate(edge_rows(n))
    ]


def edge_adjoint(*refs):
    (state_out, xb_out, far_out, near_out), scratch = refs[11:15], refs[15:]
    rows = edge_states(*refs[:11], *scratch)
    send_edges(refs[0], rows, far_out, near_out)
    for i, row in enumerate(rows):
        state_out[i] = row
        xb_out[i] = row.astype(BF16)


def last_adjoint(*refs):
    inner, out, scratch = refs[11], refs[12], refs[13:]
    c, n = out.shape[:2]
    for r in range(2, n - 2):
        out[:, r, :] = inner[r - 2][:c]
    for r, row in zip(edge_rows(n), edge_states(*refs[:11], *scratch)):
        out[:, r, :] = row[:c]


def local(first_guess, background, observed, cell_mask, chan_mask, w_in, b_in, w_out):
    c, n, lon = first_guess.shape[1:]
    hid = b_in.shape[0]
    lat, lats = lax.axis_index("lat"), lax.axis_size("lat")
    tm, tms = lax.axis_index("tm"), lax.axis_size("tm")
    odd = lat % 2 == 1
    flags = jnp.stack([lat > 0, lat < lats - 1, tm < tms - 1, tm == 0, odd]).astype(F32)
    near_pairs = [p for i in range(0, lats - 1, 2) for p in ((i, i + 1), (i + 1, i))]
    far_pairs = [p for i in range(1, lats - 1, 2) for p in ((i, i + 1), (i + 1, i))]
    ahead = [(i, i + 1) for i in range(tms - 1)]
    back = [(j, i) for i, j in ahead]

    def exchange(far, near):
        far = lax.ppermute(far, "lat", far_pairs)
        near = lax.ppermute(near, "lat", near_pairs)
        return far, near

    def shift(x, pairs):
        return lax.ppermute(x, "tm", pairs)

    cell = cell_mask[0]
    w_in = w_in.transpose(0, 2, 1)
    S = jax.ShapeDtypeStruct
    rows = S((n, CF, lon), F32)
    edge, four_f, four_b = S((2, CF, lon), BF16), S((4, CF, lon), F32), S((4, CF, lon), BF16)
    mid_f, mid_b = S((n - 4, CF, lon), F32), S((n - 4, CF, lon), BF16)
    four_h, six_h = S((4, hid, lon), BF16), S((n - 2, hid, lon), BF16)
    ups, downs = S((hid, 3 * ROW), BF16), S((3 * CF, 3 * hid), BF16)
    bias_s, chan_s = S((hid, 128), F32), S((CF, lon), F32)
    parts = S((4, hid, lon), F32), four_f
    unit = 2 * 9 * c * hid * lon

    def call(body, count, outs, held=0, work=0, flagged=True):
        return pl.pallas_call(
            body,
            out_shape=outs,
            in_specs=[SMEM] * flagged + [VMEM] * count,
            out_specs=(VMEM,) * len(outs),
            scratch_shapes=[pltpu.VMEM((8 * ROW, lon), BF16), pltpu.VMEM((held * hid, lon), BF16)] if held else [],
            compiler_params=pltpu.CompilerParams(vmem_limit_bytes=11 * 2**20),
            cost_estimate=pl.CostEstimate(flops=work * unit, bytes_accessed=4 * 2**20, transcendentals=0),
        )

    state_e, state_i, xb_e, far, near = call(prepare, 1, (four_f, mid_f, S((n, CF, lon), BF16), edge, edge))(
        flags, first_guess[0])
    for step in range(ITERS):
        far, near = exchange(far, near)
        nxt_e = shift(xb_e, back)
        if step == 0:
            nxt_i = nxt_e
            up1, dn1, obs, bias, chan = call(
                prepare_forward, 5, (ups, downs, rows, bias_s, chan_s), work=4, flagged=False
            )(w_in, w_out, observed[0], b_in[None], chan_mask)
        own = (xb_e,) if step == 0 else (xb_e, xb_i)
        fore_i, send, slope_i, *mids = call(
            first_forward if step == 0 else inner_forward, 4 + len(own),
            (mid_f, mid_b, six_h, *parts), n - 2, 10, False,
        )(*own, state_i, up1, bias, dn1)
        prev_i = shift(send, ahead)
        send, lb_e, far, near, slope_e, acc_e = call(
            edge_forward, 12, (four_b, four_b, edge, edge, four_h, four_f), 4, 8
        )(flags, far, near, *mids, state_e, obs, nxt_e, cell, chan, up1, bias, dn1)
        far, near = exchange(far, near)
        prev_e = shift(send, ahead)
        lb_i, acc_i = call(inner_misfit, 6, (mid_b, mid_f))(flags, fore_i, state_i, obs, nxt_i, cell, chan)
        if step == 0:
            up2, dn2, ground = call(
                prepare_adjoint, 3, (ups, downs, rows), work=4, flagged=False
            )(w_in, w_out, background)
        state_i, xb_i, *mids = call(
            inner_adjoint, 8, (mid_f, mid_b, *parts), n - 2, 10
        )(flags, lb_e, lb_i, slope_i, acc_i, prev_i, ground, up2, dn2)
        tail = (flags, far, near, *mids, slope_e, acc_e, prev_e, ground, up2, dn2)
        if step < ITERS - 1:
            nxt_i = shift(xb_i, back)
            state_e, xb_e, far, near = call(edge_adjoint, 10, (four_f, four_b, edge, edge), 4, 8)(*tail)
        else:
            (analysis,) = call(last_adjoint, 11, (S((c, n, lon), F32),), 4, 8)(*tail, state_i)
    return analysis[None]


def solution(mesh):
    return jax.shard_map(
        local,
        mesh=mesh,
        in_specs=(
            P("tm", None, "lat", None),
            P(None, "lat", None),
            P("tm", None, "lat", None),
            P("tm", "lat", None),
            P("tm", None),
            P(),
            P(),
            P(),
        ),
        out_specs=P("tm", None, "lat", None),
        check_vma=False,
    )
```
